32 devices in a mesh: ctx: 4 (over x, core), dp: 4 (over z), fsdp: 2 (over y).
Axes of the slice: x: 2, y: 2, z: 4, core: 2. Of those that a mesh axis runs over, the one named last changes fastest.
Arguments:
- block_input: bfloat16 [8, 1024, 1536], P(('dp', 'fsdp'), 'ctx'), may hold values from -36 to 36
- positions: int32 [8, 1024], P(('dp', 'fsdp'), 'ctx'), may hold values from 0 to 1023, as said below
- out_cotangent: bfloat16 [8, 1024, 1536], P(('dp', 'fsdp'), 'ctx'), may hold values from -6 to 6
- gain_attn: bfloat16 [1536], P(('dp', 'fsdp')), may hold values from 0.5 to 1.5
- gain_ffn: bfloat16 [1536], P(('dp', 'fsdp')), may hold values from 0.5 to 1.5
- w_query: bfloat16 [1536, 1536], P(('dp', 'fsdp')), may hold values from -0.102062073 to 0.102062073
- w_key: bfloat16 [1536, 768], P(('dp', 'fsdp')), may hold values from -0.102062073 to 0.102062073
- value_weight: bfloat16 [1536, 768], P(('dp', 'fsdp')), may hold values from -0.15625 to 0.15625
- w_output: bfloat16 [1536, 1536], P(('dp', 'fsdp')), may hold values from -0.625 to 0.625
- w_gate: bfloat16 [1536, 4096], P(('dp', 'fsdp')), may hold values from -0.15625 to 0.15625
- w_up: bfloat16 [1536, 4096], P(('dp', 'fsdp')), may hold values from -0.15625 to 0.15625
- w_down: bfloat16 [1536, 4096], P(('dp', 'fsdp')), may hold values from -0.09375 to 0.09375
Outputs:
- block_output: bfloat16 [8, 1024, 1536], P(('dp', 'fsdp'), 'ctx')
- input_grad: float32 [8, 1024, 1536], P(('dp', 'fsdp'), 'ctx')
- grad_gain_attn: float32 [1536], P(('dp', 'fsdp'))
- grad_gain_ffn: float32 [1536], P(('dp', 'fsdp'))
- grad_query: float32 [1536, 1536], P(('dp', 'fsdp'))
- grad_key: float32 [1536, 768], P(('dp', 'fsdp'))
- grad_value: float32 [1536, 768], P(('dp', 'fsdp'))
- grad_output: float32 [1536, 1536], P(('dp', 'fsdp'))
- grad_gate: float32 [1536, 4096], P(('dp', 'fsdp'))
- grad_up: float32 [1536, 4096], P(('dp', 'fsdp'))
- grad_down: float32 [1536, 4096], P(('dp', 'fsdp'))
The draws below stay inside these ranges and needn't reach their ends.
Inputs may be any that keep to these rules, and one draw needn't show every extreme that they name: In each sequence every index of ctx holds 256 consecutive ascending positions, and the sequence's positions are a permutation of 0 to 1023.
All inputs are finite; a program needn't handle non-finite values.
Results may differ from the reference program's by a relative error of at most 0.02.
Values may be sent and summed in bfloat16 or wider, within the bound.
No kernel may reach another device: no remote copies, remote signals or barrier semaphores. Data moves between devices by JAX's collectives and lax.ppermute only.
A program may use at most 448 MiB of HBM per device.

```python
import math
import jax
import jax.numpy as jnp
from jax import lax

MODEL_WIDTH = 1536
QUERY_HEADS = 16
KEY_VALUE_HEADS = 8
HEAD_SIZE = 96
FF = 4096
TOK_DEV = 256
SEQUENCE_LENGTH = 1024
SEQS = 8


def query_start(key):
    return jnp.clip(jax.random.normal(jax.random.fold_in(key, 11), (MODEL_WIDTH, QUERY_HEADS * HEAD_SIZE), jnp.float32), -4.0, 4.0) * MODEL_WIDTH ** (-0.5)


def draw_w_query(key, part):
    return query_start(key).astype(jnp.bfloat16)


def draw_w_key(key, part):
    final_result = jnp.clip(jax.random.normal(jax.random.fold_in(key, 12), (MODEL_WIDTH, KEY_VALUE_HEADS * HEAD_SIZE), jnp.float32), -4.0, 4.0) * MODEL_WIDTH ** (-0.5)
    return final_result.astype(jnp.bfloat16)


def draw_block_input(key, part):
    first, second, third = jax.random.split(key, 3)
    row_scale = jnp.exp(jax.random.uniform(first, (SEQS, SEQUENCE_LENGTH, 1), jnp.float32, math.log(0.3), math.log(3.0)))
    column_scale = jnp.exp(jax.random.uniform(second, (MODEL_WIDTH,), jnp.float32, math.log(0.3), math.log(3.0)))
    base = jnp.clip(jax.random.normal(third, (SEQS, SEQUENCE_LENGTH, MODEL_WIDTH), jnp.float32), -4.0, 4.0)
    return (base * row_scale * column_scale[None, None, :]).astype(jnp.bfloat16)


def draw_positions(key, part):
    blocks = SEQUENCE_LENGTH // TOK_DEV
    keys_all = jax.random.split(key, SEQS)
    orders = jax.vmap(lambda single: jax.random.permutation(single, blocks))(keys_all).astype(jnp.int32)
    within = jnp.arange(TOK_DEV, dtype=jnp.int32)
    return (orders[:, :, None] * TOK_DEV + within[None, None, :]).reshape(SEQS, SEQUENCE_LENGTH)


def shard_levels(key, dims, shards, low, largest):
    def one(dim, blocks):
        draws = jax.random.uniform(jax.random.fold_in(jax.random.fold_in(key, 6), dim), (blocks,), jnp.float32, low / len(shards), largest / len(shards))
        return jnp.repeat(jnp.exp(draws), dims[dim] // blocks).reshape((-1,) + (1,) * (len(dims) - dim - 1))

    loudness = one(*shards[0])
    for cut in shards[1:]:
        loudness = loudness * one(*cut)
    return loudness


def normal_values(key, extent, spread, most, cuts=(), kind=jnp.bfloat16):
    array = jax.random.normal(key, extent, jnp.float32) * spread
    if len(cuts) > 0:
        array = shard_levels(key, extent, cuts, -0.22, 0.18) * array
    return jnp.clip(array, min=-most, max=most).astype(kind)


def setup_inputs(seed: int = 0) -> dict:
    key_list = jax.random.split(jax.random.key(seed), 13)
    return {
        "block_input": draw_block_input(jax.random.fold_in(key_list[12], 71), 0),
        "positions": draw_positions(jax.random.fold_in(key_list[12], 71), 0),
        "out_cotangent": normal_values(key_list[2], (SEQS, SEQUENCE_LENGTH, MODEL_WIDTH), 1.0, 6.0, ((0, 8), (1, 4))),
        "gain_attn": jnp.clip(1.0 + 0.1 * jax.random.normal(key_list[3], (MODEL_WIDTH,), jnp.float32), 0.5, 1.5).astype(jnp.bfloat16),
        "gain_ffn": jnp.clip(1.0 + 0.1 * jax.random.normal(key_list[4], (MODEL_WIDTH,), jnp.float32), 0.5, 1.5).astype(jnp.bfloat16),
        "w_query": draw_w_query(jax.random.fold_in(key_list[12], 71), 0),
        "w_key": draw_w_key(jax.random.fold_in(key_list[12], 71), 0),
        "value_weight": normal_values(key_list[7], (MODEL_WIDTH, KEY_VALUE_HEADS * HEAD_SIZE), MODEL_WIDTH ** -0.5, 0.15625, ((0, 8),)),
        "w_output": normal_values(key_list[8], (MODEL_WIDTH, QUERY_HEADS * HEAD_SIZE), (QUERY_HEADS * HEAD_SIZE // 16) ** -0.5, 0.625, ((0, 8),)),
        "w_gate": normal_values(key_list[9], (MODEL_WIDTH, FF), MODEL_WIDTH ** -0.5, 0.15625, ((0, 8),)),
        "w_up": normal_values(key_list[10], (MODEL_WIDTH, FF), MODEL_WIDTH ** -0.5, 0.15625, ((0, 8),)),
        "w_down": normal_values(key_list[11], (MODEL_WIDTH, FF), FF ** -0.5, 0.09375, ((0, 8),)),
    }


EPSILON = 1e-05
THETA = 100000.0
MASK_FLOOR = -1e+30

def rope_tables(order_pos, head_dim):
    half_dim = head_dim // 2
    frequency = THETA ** (-(jnp.arange(half_dim, dtype=jnp.float32) * 2.0) / head_dim)
    angles = order_pos.astype(jnp.float32)[:, None] * frequency[None, :]
    angles = jnp.concatenate([angles, angles], axis=1)
    return (jnp.cos(angles), jnp.sin(angles))

def rotate_half(values):
    half_dim = values.shape[-1] // 2
    return jnp.concatenate([-values[..., half_dim:], values[..., :half_dim]], axis=-1)

def apply_rotary(values, cosine_table, sine_values):
    return values * cosine_table[:, None, :] + rotate_half(values) * sine_values[:, None, :]

def inverse_rotary(gradient, cosine_table, sine_values):
    return gradient * cosine_table[:, None, :] - rotate_half(gradient) * sine_values[:, None, :]

def times_t(left, right):
    return lax.dot_general(left, right, (((1,), (1,)), ((), ())), preferred_element_type=jnp.float32)

def left_t(left, right):
    return lax.dot_general(left, right, (((0,), (0,)), ((), ())), preferred_element_type=jnp.float32)

def norm_backward(upstream, gain_full, normed, inverse):
    scaled = upstream * gain_full[None, :]
    return inverse * (scaled - normed * lax.optimization_barrier(jnp.mean(scaled * normed, axis=1, keepdims=True)))

def reference(block_input, positions, out_cotangent, gain_attn, gain_ffn, w_query, w_key, value_weight, w_output, w_gate, w_up, w_down):
    query_groups = QUERY_HEADS // KEY_VALUE_HEADS
    scale = HEAD_SIZE ** (-0.5)
    current_query_block = math.gcd(SEQUENCE_LENGTH, 512)
    block_count = SEQUENCE_LENGTH // current_query_block
    gain_first = gain_attn.astype(jnp.float32)
    gain_second = gain_ffn.astype(jnp.float32)
    qwidth = QUERY_HEADS * HEAD_SIZE
    key_width = KEY_VALUE_HEADS * HEAD_SIZE

    def sequence(carry, inputs):
        x_seq, order_seq, cotangent = inputs
        values_in = x_seq.astype(jnp.float32)
        inverse_one = lax.rsqrt(lax.optimization_barrier(jnp.mean(values_in * values_in, axis=1, keepdims=True)) + EPSILON)
        norm_one = values_in * inverse_one
        normed_one = (norm_one * gain_first[None, :]).astype(jnp.bfloat16)
        query_matrix = jnp.dot(normed_one, w_query, preferred_element_type=jnp.float32)
        projected_keys = jnp.dot(normed_one, w_key, preferred_element_type=jnp.float32)
        projected_values = jnp.dot(normed_one, value_weight, preferred_element_type=jnp.float32)
        cosine_table, sine_values = rope_tables(order_seq, HEAD_SIZE)
        rotated_query = apply_rotary(query_matrix.reshape(SEQUENCE_LENGTH, QUERY_HEADS, HEAD_SIZE), cosine_table, sine_values).astype(jnp.bfloat16).reshape(SEQUENCE_LENGTH, KEY_VALUE_HEADS, query_groups, HEAD_SIZE)
        rotated_key = apply_rotary(projected_keys.reshape(SEQUENCE_LENGTH, KEY_VALUE_HEADS, HEAD_SIZE), cosine_table, sine_values).astype(jnp.bfloat16)
        value_block_rows = projected_values.reshape(SEQUENCE_LENGTH, KEY_VALUE_HEADS, HEAD_SIZE).astype(jnp.bfloat16)
        key_f = rotated_key.astype(jnp.float32)
        value_f = value_block_rows.astype(jnp.float32)
        query_block_list = rotated_query.reshape(block_count, current_query_block, KEY_VALUE_HEADS, query_groups, HEAD_SIZE)
        order_blocks = order_seq.reshape(block_count, current_query_block)

        def scores_of(query_block, order_block):
            scores = jnp.einsum('qhgd,khd->hgqk', query_block.astype(jnp.float32), key_f) * scale
            visible = order_seq[None, None, None, :] <= order_block[None, None, :, None]
            return (jnp.where(visible, scores, MASK_FLOOR), visible)

        def attend(pair):
            query_block, order_block = pair
            scores, visible = scores_of(query_block, order_block)
            row_max = lax.optimization_barrier(jnp.max(scores, axis=3))
            expo = jnp.where(visible, jnp.exp(scores - row_max[..., None]), 0.0)
            row_sum = lax.optimization_barrier(jnp.sum(expo, axis=3))
            output = jnp.einsum('hgqk,khd->qhgd', expo.astype(jnp.bfloat16).astype(jnp.float32), value_f)
            output = output / jnp.transpose(row_sum, (2, 0, 1))[..., None]
            return (output, row_max + jnp.log(row_sum))
        outs_blocks, lse_blocks = lax.map(attend, (query_block_list, order_blocks))
        attention_output = outs_blocks.reshape(SEQUENCE_LENGTH, qwidth).astype(jnp.bfloat16)
        mid = values_in + times_t(attention_output, w_output)
        inverse_two = lax.rsqrt(lax.optimization_barrier(jnp.mean(mid * mid, axis=1, keepdims=True)) + EPSILON)
        norm_two = mid * inverse_two
        normed_two = (norm_two * gain_second[None, :]).astype(jnp.bfloat16)
        gate = jnp.dot(normed_two, w_gate, preferred_element_type=jnp.float32)
        upper = jnp.dot(normed_two, w_up, preferred_element_type=jnp.float32)
        sigma = jax.nn.sigmoid(gate)
        silu_gate = gate * sigma
        hidden = (silu_gate * upper).astype(jnp.bfloat16)
        output_seq = (mid + times_t(hidden, w_down)).astype(jnp.bfloat16)
        d_hidden = jnp.dot(cotangent, w_down, preferred_element_type=jnp.float32)
        d_gate = (d_hidden * upper * sigma * (1.0 + gate * (1.0 - sigma))).astype(jnp.bfloat16)
        d_upper = (d_hidden * silu_gate).astype(jnp.bfloat16)
        d_normed_two = times_t(d_gate, w_gate) + times_t(d_upper, w_up)
        d_mid = cotangent.astype(jnp.float32) + norm_backward(d_normed_two, gain_second, norm_two, inverse_two)
        d_mid_b = d_mid.astype(jnp.bfloat16)
        attention_output_gradient = jnp.dot(d_mid_b, w_output, preferred_element_type=jnp.float32)
        block_output_gradient = attention_output_gradient.astype(jnp.bfloat16).reshape(block_count, current_query_block, KEY_VALUE_HEADS, query_groups, HEAD_SIZE)
        attention_block_outputs = attention_output.reshape(block_count, current_query_block, KEY_VALUE_HEADS, query_groups, HEAD_SIZE)

        def backward_block(grads, inputs_block):
            d_key, d_value = grads
            query_block, order_block, dout_block, att_block, lse_block = inputs_block
            dout_f = dout_block.astype(jnp.float32)
            delta = jnp.transpose(lax.optimization_barrier(jnp.sum(dout_f * att_block.astype(jnp.float32), axis=3)), (1, 2, 0))
            scores, visible = scores_of(query_block, order_block)
            probs = jnp.where(visible, jnp.exp(scores - lse_block[..., None]), 0.0)
            d_probs = jnp.einsum('qhgd,khd->hgqk', dout_f, value_f)
            d_scores = (probs * (d_probs - delta[..., None]) * scale).astype(jnp.bfloat16).astype(jnp.float32)
            query_gradient = jnp.einsum('hgqk,khd->qhgd', d_scores, key_f)
            d_key = d_key + jnp.einsum('hgqk,qhgd->khd', d_scores, query_block.astype(jnp.float32))
            d_value = d_value + jnp.einsum('hgqk,qhgd->khd', probs.astype(jnp.bfloat16).astype(jnp.float32), dout_f)
            return ((d_key, d_value), query_gradient)
        zero_key_value = jnp.zeros((SEQUENCE_LENGTH, KEY_VALUE_HEADS, HEAD_SIZE), jnp.float32)
        (d_key, d_value), query_gradient = lax.scan(backward_block, (zero_key_value, zero_key_value), (query_block_list, order_blocks, block_output_gradient, attention_block_outputs, lse_blocks))
        d_query_pre = inverse_rotary(query_gradient.reshape(SEQUENCE_LENGTH, QUERY_HEADS, HEAD_SIZE), cosine_table, sine_values).reshape(SEQUENCE_LENGTH, qwidth)
        unrotated_key_gradient = inverse_rotary(d_key, cosine_table, sine_values).reshape(SEQUENCE_LENGTH, key_width)
        d_query_b = d_query_pre.astype(jnp.bfloat16)
        d_key_b = unrotated_key_gradient.astype(jnp.bfloat16)
        d_value_b = d_value.reshape(SEQUENCE_LENGTH, key_width).astype(jnp.bfloat16)
        d_normed_one = times_t(d_query_b, w_query) + times_t(d_key_b, w_key) + times_t(d_value_b, value_weight)
        grad_seq = d_mid + norm_backward(d_normed_one, gain_first, norm_one, inverse_one)
        terms = (left_t(normed_one, d_query_b), left_t(normed_one, d_key_b), left_t(normed_one, d_value_b), left_t(d_mid_b, attention_output), left_t(normed_two, d_gate), left_t(normed_two, d_upper), left_t(cotangent, hidden))
        carry = tuple((total_now + term for total_now, term in zip(carry, terms)))
        return (carry, (output_seq, grad_seq))
    init = (jnp.zeros((MODEL_WIDTH, qwidth), jnp.float32), jnp.zeros((MODEL_WIDTH, key_width), jnp.float32), jnp.zeros((MODEL_WIDTH, key_width), jnp.float32), jnp.zeros((MODEL_WIDTH, qwidth), jnp.float32), jnp.zeros((MODEL_WIDTH, FF), jnp.float32), jnp.zeros((MODEL_WIDTH, FF), jnp.float32), jnp.zeros((MODEL_WIDTH, FF), jnp.float32))
    totals, (block_output, input_grad) = lax.scan(sequence, init, (block_input, positions, out_cotangent))
    grad_query, grad_key, grad_value, grad_output, grad_gate, grad_up, grad_down = totals
    grad_gain_attn = (lax.optimization_barrier(jnp.sum(w_query.astype(jnp.float32) * grad_query, axis=1)) + lax.optimization_barrier(jnp.sum(w_key.astype(jnp.float32) * grad_key, axis=1)) + lax.optimization_barrier(jnp.sum(value_weight.astype(jnp.float32) * grad_value, axis=1))) / gain_first
    grad_gain_ffn = (lax.optimization_barrier(jnp.sum(w_gate.astype(jnp.float32) * grad_gate, axis=1)) + lax.optimization_barrier(jnp.sum(w_up.astype(jnp.float32) * grad_up, axis=1))) / gain_second
    return (block_output, input_grad, grad_gain_attn, grad_gain_ffn, grad_query, grad_key, grad_value, grad_output, grad_gate, grad_up, grad_down)
```

```python
import jax
import jax.numpy as jnp
from jax import lax
from jax.sharding import PartitionSpec as P

QUERY_HEADS = 16
KEY_VALUE_HEADS = 8
HEAD_SIZE = 96
FF = 4096

EPSILON = 1e-05
THETA = 100000.0
MASK_FLOOR = -1e30
ROWS = ("dp", "fsdp")


def rope_tables(order_pos, head_dim):
    half_dim = head_dim // 2
    frequency = THETA ** (-(jnp.arange(half_dim, dtype=jnp.float32) * 2.0) / head_dim)
    angles = order_pos.astype(jnp.float32)[:, None] * frequency[None, :]
    angles = jnp.concatenate([angles, angles], axis=1)
    return (jnp.cos(angles), jnp.sin(angles))


def rotate_half(values):
    half_dim = values.shape[-1] // 2
    return jnp.concatenate([-values[..., half_dim:], values[..., :half_dim]], axis=-1)


def apply_rotary(values, cosine_table, sine_values):
    return values * cosine_table[:, None, :] + rotate_half(values) * sine_values[:, None, :]


def inverse_rotary(gradient, cosine_table, sine_values):
    return gradient * cosine_table[:, None, :] - rotate_half(gradient) * sine_values[:, None, :]


def times(left, right):
    return jnp.dot(left, right, preferred_element_type=jnp.float32)


def times_t(left, right):
    return lax.dot_general(
        left, right, (((1,), (1,)), ((), ())), preferred_element_type=jnp.float32
    )


def left_t(left, right):
    return lax.dot_general(
        left, right, (((0,), (0,)), ((), ())), preferred_element_type=jnp.float32
    )


def norm_backward(upstream, gain_full, normed, inverse):
    scaled = upstream * gain_full[None, :]
    return inverse * (scaled - normed * jnp.mean(scaled * normed, axis=1, keepdims=True))


def flip(array, bit, count):
    return lax.ppermute(array, "ctx", [(i, i ^ bit) for i in range(count)])


def bits_of(count):
    return [1 << k for k in range(count.bit_length() - 1)]


def gather_ctx(own, count):
    blocks = {0: own}
    for bit in reversed(bits_of(count)):
        for j in list(blocks):
            blocks[j | bit] = flip(blocks[j], bit, count)
    return [blocks[j] for j in range(count)]


def reduce_ctx(blocks, count):
    totals = list(blocks)
    for bit in bits_of(count):
        for j in range(0, count, 2 * bit):
            moved = flip(totals[j | bit].astype(jnp.bfloat16), bit, count)
            totals[j] = totals[j].astype(jnp.float32) + moved.astype(jnp.float32)
    return totals[0]


def canonical(blocks, index):
    for bit in bits_of(len(blocks)):
        swap = (index & bit) != 0
        blocks = [jnp.where(swap, blocks[j ^ bit], blocks[j]) for j in range(len(blocks))]
    return blocks


def rows_scatter(part):
    return lax.psum_scatter(part.astype(jnp.bfloat16), ROWS, scatter_dimension=0, tiled=True)


def make(count):
    q_heads = QUERY_HEADS // count
    kv_heads = KEY_VALUE_HEADS // count
    groups = q_heads // kv_heads
    q_cols, kv_cols, ff_cols = q_heads * HEAD_SIZE, kv_heads * HEAD_SIZE, FF // count
    scale = HEAD_SIZE ** (-0.5)

    def shards(
        block_input,
        positions,
        out_cotangent,
        gain_attn,
        gain_ffn,
        w_query,
        w_key,
        value_weight,
        w_output,
        w_gate,
        w_up,
        w_down,
    ):
        tokens = block_input.shape[1]
        every = tokens * count
        index = lax.axis_index("ctx")

        def mine(weight, width):
            return lax.dynamic_slice_in_dim(weight, index * width, width, axis=1)

        gains = jnp.pad(jnp.stack([gain_attn, gain_ffn], axis=1), ((0, 0), (0, 126)))
        attn_part = jnp.concatenate(
            [
                mine(w_query, q_cols),
                mine(w_key, kv_cols),
                mine(value_weight, kv_cols),
                mine(w_output, q_cols),
                gains,
            ],
            axis=1,
        )
        attn_full = lax.all_gather(attn_part, ROWS, axis=0, tiled=True)
        ffn_part = jnp.concatenate(
            [mine(w_gate, ff_cols), mine(w_up, ff_cols), mine(w_down, ff_cols)], axis=1
        )
        ffn_full = lax.all_gather(ffn_part, ROWS, axis=0, tiled=True)

        own_x = block_input[0]
        x_all = jnp.concatenate(gather_ctx(own_x, count), axis=0)
        order_all = jnp.concatenate(gather_ctx(positions[0], count), axis=0)
        cotangent = out_cotangent[0]
        cot_all = jnp.concatenate(gather_ctx(cotangent, count), axis=0)

        qkv_cols = q_cols + 2 * kv_cols
        w_qkv = attn_full[:, :qkv_cols]
        w_o = attn_full[:, qkv_cols : qkv_cols + q_cols]
        gain_first = attn_full[:, qkv_cols + q_cols].astype(jnp.float32)
        gain_second = attn_full[:, qkv_cols + q_cols + 1].astype(jnp.float32)

        values_in = x_all.astype(jnp.float32)
        inverse_one = lax.rsqrt(jnp.mean(values_in * values_in, axis=1, keepdims=True) + EPSILON)
        normed_one = (values_in * inverse_one * gain_first[None, :]).astype(jnp.bfloat16)
        qkv = times(normed_one, w_qkv)
        cosine_table, sine_values = rope_tables(order_all, HEAD_SIZE)
        query = (
            apply_rotary(qkv[:, :q_cols].reshape(every, q_heads, HEAD_SIZE), cosine_table, sine_values)
            .astype(jnp.bfloat16)
            .reshape(every, kv_heads, groups, HEAD_SIZE)
        )
        key = apply_rotary(
            qkv[:, q_cols : q_cols + kv_cols].reshape(every, kv_heads, HEAD_SIZE),
            cosine_table,
            sine_values,
        ).astype(jnp.bfloat16)
        value = qkv[:, q_cols + kv_cols :].astype(jnp.bfloat16).reshape(every, kv_heads, HEAD_SIZE)
        visible = (order_all[None, :] <= order_all[:, None])[None, None]

        def score():
            raw = jnp.einsum("qhgd,khd->hgqk", query, key, preferred_element_type=jnp.float32)
            return jnp.where(visible, raw * scale, MASK_FLOOR)

        scores = score()
        row_max = jnp.max(scores, axis=3)
        weights = jnp.where(visible, jnp.exp(scores - row_max[..., None]), 0.0)
        row_sum = jnp.sum(weights, axis=3)
        lse = row_max + jnp.log(row_sum)
        attended_heads = jnp.einsum(
            "hgqk,khd->hgqd", weights.astype(jnp.bfloat16), value, preferred_element_type=jnp.float32
        )
        attended = (
            jnp.transpose(attended_heads / row_sum[..., None], (2, 0, 1, 3))
            .reshape(every, q_cols)
            .astype(jnp.bfloat16)
        )

        def split(full):
            return [full[j * tokens : (j + 1) * tokens] for j in range(count)]

        projected = reduce_ctx(split(times_t(attended, w_o)), count)
        own_values = own_x.astype(jnp.float32)
        mid = own_values + projected
        inverse_two = lax.rsqrt(jnp.mean(mid * mid, axis=1, keepdims=True) + EPSILON)
        norm_two = mid * inverse_two
        normed_two = jnp.concatenate(
            gather_ctx((norm_two * gain_second[None, :]).astype(jnp.bfloat16), count), axis=0
        )

        w_gu = ffn_full[:, : 2 * ff_cols]
        w_d = ffn_full[:, 2 * ff_cols :]
        gate_up = times(normed_two, w_gu)
        d_hidden = times(cot_all, w_d)
        gate, up = gate_up[:, :ff_cols], gate_up[:, ff_cols:]
        sigma = jax.nn.sigmoid(gate)
        silu_gate = gate * sigma
        hidden = (silu_gate * up).astype(jnp.bfloat16)
        d_gate = (d_hidden * up * sigma * (1.0 + gate * (1.0 - sigma))).astype(jnp.bfloat16)
        d_up = (d_hidden * silu_gate).astype(jnp.bfloat16)
        d_gate_up = jnp.concatenate([d_gate, d_up], axis=1)
        d_normed_two = reduce_ctx(split(times_t(d_gate_up, w_gu)), count)
        d_mid = cotangent.astype(jnp.float32) + norm_backward(
            d_normed_two, gain_second, norm_two, inverse_two
        )
        d_mid_b = jnp.concatenate(gather_ctx(d_mid.astype(jnp.bfloat16), count), axis=0)

        grad_gu_rows = rows_scatter(left_t(normed_two, d_gate_up))
        grad_d_rows = rows_scatter(left_t(cot_all, hidden))
        block_output = (mid + reduce_ctx(split(times_t(hidden, w_d)), count)).astype(jnp.bfloat16)

        d_attended = times(d_mid_b, w_o).astype(jnp.bfloat16)
        d_out = d_attended.reshape(every, kv_heads, groups, HEAD_SIZE)
        delta = jnp.transpose(
            jnp.sum(
                d_out.astype(jnp.float32)
                * attended.reshape(every, kv_heads, groups, HEAD_SIZE).astype(jnp.float32),
                axis=3,
            ),
            (1, 2, 0),
        )
        probs = jnp.where(visible, jnp.exp(score() - lse[..., None]), 0.0)
        d_probs = jnp.einsum("qhgd,khd->hgqk", d_out, value, preferred_element_type=jnp.float32)
        d_scores = (probs * (d_probs - delta[..., None]) * scale).astype(jnp.bfloat16)
        d_query = jnp.einsum("hgqk,khd->qhgd", d_scores, key, preferred_element_type=jnp.float32)
        d_key = jnp.einsum("hgqk,qhgd->khd", d_scores, query, preferred_element_type=jnp.float32)
        d_value = jnp.einsum(
            "hgqk,qhgd->khd", probs.astype(jnp.bfloat16), d_out, preferred_element_type=jnp.float32
        ).reshape(every, kv_cols)
        d_query_pre = inverse_rotary(
            d_query.reshape(every, q_heads, HEAD_SIZE), cosine_table, sine_values
        ).reshape(every, q_cols)
        d_key_pre = inverse_rotary(d_key, cosine_table, sine_values).reshape(every, kv_cols)
        d_qkv = jnp.concatenate([d_query_pre, d_key_pre, d_value], axis=1).astype(jnp.bfloat16)
        d_normed_one = reduce_ctx(split(times_t(d_qkv, w_qkv)), count)
        own_inverse = inverse_one[:tokens]
        input_grad = d_mid + norm_backward(
            d_normed_one, gain_first, own_values * own_inverse, own_inverse
        )

        grad_attn_rows = rows_scatter(
            jnp.concatenate([left_t(normed_one, d_qkv), left_t(d_mid_b, attended)], axis=1)
        )

        def spread(rows):
            return canonical(gather_ctx(rows, count), index)

        def joined(blocks, start, width):
            return jnp.concatenate(
                [b[:, start : start + width] for b in blocks], axis=1
            ).astype(jnp.float32)

        gu_blocks = spread(grad_gu_rows)
        grad_gate = joined(gu_blocks, 0, ff_cols)
        grad_up = joined(gu_blocks, ff_cols, ff_cols)
        grad_down = joined(spread(grad_d_rows), 0, ff_cols)
        attn_blocks = spread(grad_attn_rows)
        grad_query = joined(attn_blocks, 0, q_cols)
        grad_key = joined(attn_blocks, q_cols, kv_cols)
        grad_value = joined(attn_blocks, q_cols + kv_cols, kv_cols)
        grad_output = joined(attn_blocks, qkv_cols, q_cols)

        grad_gain_attn = (
            jnp.sum(w_query.astype(jnp.float32) * grad_query, axis=1)
            + jnp.sum(w_key.astype(jnp.float32) * grad_key, axis=1)
            + jnp.sum(value_weight.astype(jnp.float32) * grad_value, axis=1)
        ) / gain_attn.astype(jnp.float32)
        grad_gain_ffn = (
            jnp.sum(w_gate.astype(jnp.float32) * grad_gate, axis=1)
            + jnp.sum(w_up.astype(jnp.float32) * grad_up, axis=1)
        ) / gain_ffn.astype(jnp.float32)
        return (
            block_output[None],
            input_grad[None],
            grad_gain_attn,
            grad_gain_ffn,
            grad_query,
            grad_key,
            grad_value,
            grad_output,
            grad_gate,
            grad_up,
            grad_down,
        )

    return shards


def solution(mesh):
    token, rows, matrix = P(ROWS, "ctx", None), P(ROWS), P(ROWS, None)
    return jax.shard_map(
        make(mesh.shape["ctx"]),
        mesh=mesh,
        in_specs=(token, P(ROWS, "ctx"), token, rows, rows) + (matrix,) * 7,
        out_specs=(token, token, rows, rows) + (matrix,) * 7,
        check_vma=False,
    )
```

```python
import functools
import math

import jax
import jax.numpy as jnp
from jax import lax
from jax.experimental import pallas as pl
from jax.experimental.pallas import tpu as pltpu
from jax.sharding import PartitionSpec as P

QUERY_HEADS = 16
KEY_VALUE_HEADS = 8
HEAD_SIZE = 96
FF = 4096

EPSILON = 1e-05
THETA = 100000.0
MASK_FLOOR = -1e30
ROWS = ("dp", "fsdp")


def rope_tables(order_pos, head_dim):
    half_dim = head_dim // 2
    frequency = THETA ** (-(jnp.arange(half_dim, dtype=jnp.float32) * 2.0) / head_dim)
    angles = frequency[:, None] * order_pos.astype(jnp.float32)[None, :]
    return (jnp.cos(angles), jnp.sin(angles))


def times(left, right):
    return jnp.dot(left, right, preferred_element_type=jnp.float32)


def times_t(left, right):
    return lax.dot_general(
        left, right, (((1,), (1,)), ((), ())), preferred_element_type=jnp.float32
    )


def left_t(left, right):
    return lax.dot_general(
        left, right, (((0,), (0,)), ((), ())), preferred_element_type=jnp.float32
    )


def dot(left, right, left_dim, right_dim):
    return lax.dot_general(
        left, right, (((left_dim,), (right_dim,)), ((), ())), preferred_element_type=jnp.float32
    )


def block_offsets(order_ref, block):
    count = order_ref.shape[0] // block
    ranks = [lax.div(order_ref[j * block], jnp.int32(block)) for j in range(count)]
    slots = [sum(jnp.where(ranks[j] == r, j, 0) for j in range(count)) for r in range(count)]
    return [pl.multiple_of(slot * block, block) for slot in slots]


def hidden_keys(block):
    rows = lax.broadcasted_iota(jnp.int32, (block, block), 0)
    columns = lax.broadcasted_iota(jnp.int32, (block, block), 1)
    return rows > columns


def score_blocks(keys_ref, key_rows, query, rank, block):
    blocks = []
    for b in range(rank + 1):
        keys = keys_ref[key_rows, b * block : (b + 1) * block]
        raw = dot(keys, query, 0, 0) * (HEAD_SIZE**-0.5 * math.log2(math.e))
        blocks.append(jnp.where(hidden_keys(block), MASK_FLOOR, raw) if b == rank else raw)
    return blocks


def attend_kernel(
    q_heads, groups, block, order_ref, qkv_ref, cos_ref, sin_ref, sorted_ref, out_ref, lse_ref
):
    offsets = block_offsets(order_ref, block)
    kv_heads = q_heads // groups
    half = HEAD_SIZE // 2
    for rank, offset in enumerate(offsets):
        here, there = pl.ds(offset, block), slice(rank * block, (rank + 1) * block)
        cosine, sine = cos_ref[:, here], sin_ref[:, here]
        for head in range(q_heads + kv_heads):
            low = slice(head * HEAD_SIZE, head * HEAD_SIZE + half)
            high = slice(head * HEAD_SIZE + half, (head + 1) * HEAD_SIZE)
            first, second = qkv_ref[low, here], qkv_ref[high, here]
            sorted_ref[low, there] = (first * cosine - second * sine).astype(jnp.bfloat16)
            sorted_ref[high, there] = (second * cosine + first * sine).astype(jnp.bfloat16)
        values = slice((q_heads + kv_heads) * HEAD_SIZE, (q_heads + 2 * kv_heads) * HEAD_SIZE)
        sorted_ref[values, there] = qkv_ref[values, here].astype(jnp.bfloat16)

    @pl.loop(0, q_heads)
    def _(head):
        rows = pl.ds(pl.multiple_of(head * HEAD_SIZE, HEAD_SIZE), HEAD_SIZE)
        group = lax.div(head, jnp.int32(groups))
        key_rows = pl.ds(pl.multiple_of((q_heads + group) * HEAD_SIZE, HEAD_SIZE), HEAD_SIZE)
        value_rows = pl.ds(
            pl.multiple_of((q_heads + kv_heads + group) * HEAD_SIZE, HEAD_SIZE), HEAD_SIZE
        )
        for rank, offset in enumerate(offsets):
            query = sorted_ref[rows, rank * block : (rank + 1) * block]
            scores = score_blocks(sorted_ref, key_rows, query, rank, block)
            row_max = functools.reduce(
                jnp.maximum, [jnp.max(s, axis=0, keepdims=True) for s in scores]
            )
            total, output = 0.0, 0.0
            for b, part in enumerate(scores):
                probs = jnp.exp2(part - row_max)
                total = total + jnp.sum(probs, axis=0, keepdims=True)
                values = sorted_ref[value_rows, b * block : (b + 1) * block]
                output = output + dot(values, probs.astype(jnp.bfloat16), 1, 0)
            out_ref[rows, pl.ds(offset, block)] = (output / total).astype(jnp.bfloat16)
            lse_ref[head, :, rank * block : (rank + 1) * block] = row_max + jnp.log2(total)


def attend_backward_kernel(
    q_heads,
    groups,
    block,
    order_ref,
    sorted_ref,
    lse_ref,
    out_ref,
    d_out_ref,
    cos_ref,
    sin_ref,
    d_qkv_ref,
    d_key_ref,
    d_value_ref,
):
    offsets = block_offsets(order_ref, block)
    kv_heads = q_heads // groups
    half = HEAD_SIZE // 2

    def unrotate(grad, base, offset):
        here = pl.ds(offset, block)
        cosine, sine = cos_ref[:, here], sin_ref[:, here]
        first, second = grad[:half], grad[half:]
        d_qkv_ref[pl.ds(pl.multiple_of(base, 16), half), here] = (
            first * cosine + second * sine
        ).astype(jnp.bfloat16)
        d_qkv_ref[pl.ds(pl.multiple_of(base + half, 16), half), here] = (
            second * cosine - first * sine
        ).astype(jnp.bfloat16)

    @pl.loop(0, kv_heads)
    def _(group):
        key_base = pl.multiple_of((q_heads + group) * HEAD_SIZE, HEAD_SIZE)
        value_base = pl.multiple_of((q_heads + kv_heads + group) * HEAD_SIZE, HEAD_SIZE)
        key_rows, value_rows = pl.ds(key_base, HEAD_SIZE), pl.ds(value_base, HEAD_SIZE)
        d_key_ref[...] = jnp.zeros_like(d_key_ref)
        d_value_ref[...] = jnp.zeros_like(d_value_ref)

        @pl.loop(0, groups)
        def _(member):
            head = group * groups + member
            base = pl.multiple_of(head * HEAD_SIZE, HEAD_SIZE)
            rows = pl.ds(base, HEAD_SIZE)
            for rank, offset in enumerate(offsets):
                here, there = pl.ds(offset, block), slice(rank * block, (rank + 1) * block)
                query = sorted_ref[rows, there]
                d_out = d_out_ref[rows, here]
                delta = jnp.sum(
                    d_out.astype(jnp.float32) * out_ref[rows, here].astype(jnp.float32),
                    axis=0,
                    keepdims=True,
                )
                lse = lse_ref[head, :, there]
                d_query = 0.0
                for b, part in enumerate(
                    score_blocks(sorted_ref, key_rows, query, rank, block)
                ):
                    span = slice(b * block, (b + 1) * block)
                    probs = jnp.exp2(part - lse)
                    d_probs = dot(sorted_ref[value_rows, span], d_out, 0, 0)
                    d_scores = (probs * (d_probs - delta) * HEAD_SIZE**-0.5).astype(jnp.bfloat16)
                    d_query = d_query + dot(sorted_ref[key_rows, span], d_scores, 1, 0)
                    d_key_ref[:, span] += dot(query, d_scores, 1, 1)
                    d_value_ref[:, span] += dot(d_out, probs.astype(jnp.bfloat16), 1, 1)
                unrotate(d_query, base, offset)

        for rank, offset in enumerate(offsets):
            there = slice(rank * block, (rank + 1) * block)
            unrotate(d_key_ref[:, there], key_base, offset)
            d_qkv_ref[value_rows, pl.ds(offset, block)] = d_value_ref[:, there].astype(jnp.bfloat16)


def attention_calls(q_heads, groups, block, every):
    rows = (q_heads + 2 * (q_heads // groups)) * HEAD_SIZE
    in_vmem, in_smem = pl.BlockSpec(memory_space=pltpu.VMEM), pl.BlockSpec(memory_space=pltpu.SMEM)
    pairs = q_heads * every * (every + block) // 2
    forward = pl.pallas_call(
        functools.partial(attend_kernel, q_heads, groups, block),
        out_shape=(
            jax.ShapeDtypeStruct((rows, every), jnp.bfloat16),
            jax.ShapeDtypeStruct((q_heads * HEAD_SIZE, every), jnp.bfloat16),
            jax.ShapeDtypeStruct((q_heads, 1, every), jnp.float32),
        ),
        in_specs=[in_smem] + [in_vmem] * 3,
        out_specs=(in_vmem,) * 3,
        cost_estimate=pl.CostEstimate(
            flops=4 * pairs * HEAD_SIZE, transcendentals=pairs, bytes_accessed=8 * rows * every
        ),
        name="attend",
    )
    backward = pl.pallas_call(
        functools.partial(attend_backward_kernel, q_heads, groups, block),
        out_shape=jax.ShapeDtypeStruct((rows, every), jnp.bfloat16),
        in_specs=[in_smem] + [in_vmem] * 6,
        out_specs=in_vmem,
        scratch_shapes=[pltpu.VMEM((HEAD_SIZE, every), jnp.float32)] * 2,
        cost_estimate=pl.CostEstimate(
            flops=10 * pairs * HEAD_SIZE, transcendentals=pairs, bytes_accessed=8 * rows * every
        ),
        name="attend_backward",
    )
    return forward, backward


def norm_backward(upstream, gain_full, normed, inverse):
    scaled = upstream * gain_full[None, :]
    return inverse * (scaled - normed * jnp.mean(scaled * normed, axis=1, keepdims=True))


def bits_of(count):
    return [1 << k for k in range(count.bit_length() - 1)]


class Cube:
    def __init__(self, mesh, axes):
        self.count, self.axes, self.steps = 1, axes, []
        for axis in reversed(axes):
            size = mesh.shape[axis]
            self.steps += [(axis, size, bit, bit * self.count) for bit in bits_of(size)]
            self.count *= size

    def index(self):
        return lax.axis_index(self.axes)

    def gather(self, own):
        blocks = {0: own}
        for axis, size, bit, offset in reversed(self.steps):
            for j in list(blocks):
                blocks[j | offset] = flip(blocks[j], axis, size, bit)
        return [blocks[j] for j in range(self.count)]

    def reduce(self, blocks):
        totals = dict(enumerate(blocks))
        for axis, size, bit, offset in self.steps:
            for j in [j for j in totals if j & offset]:
                moved = flip(totals.pop(j).astype(jnp.bfloat16), axis, size, bit)
                totals[j ^ offset] = totals[j ^ offset].astype(jnp.float32) + moved.astype(
                    jnp.float32
                )
        return totals[0]

    def gather_rows(self, part):
        rows, columns = part.shape
        full = jnp.zeros((rows * self.count, columns), part.dtype)
        for j, block in enumerate(self.gather(part)):
            full = lax.dynamic_update_slice(full, block, ((self.index() ^ j) * rows, 0))
        return full

    def reduce_rows(self, full):
        rows = full.shape[0] // self.count
        full = full.astype(jnp.bfloat16)
        return self.reduce(
            [
                lax.dynamic_slice_in_dim(full, (self.index() ^ j) * rows, rows, axis=0)
                for j in range(self.count)
            ]
        ).astype(jnp.bfloat16)


def flip(array, axis, size, bit):
    return lax.ppermute(array, axis, [(i, i ^ bit) for i in range(size)])


def canonical(blocks, index):
    for bit in bits_of(len(blocks)):
        swap = (index & bit) != 0
        blocks = [jnp.where(swap, blocks[j ^ bit], blocks[j]) for j in range(len(blocks))]
    return blocks


def rows_scatter(part):
    return lax.psum_scatter(part.astype(jnp.bfloat16), ROWS, scatter_dimension=0, tiled=True)


def make(mesh):
    ctx, grid = Cube(mesh, ("ctx",)), Cube(mesh, ROWS)
    count = ctx.count
    q_heads = QUERY_HEADS // count
    kv_heads = KEY_VALUE_HEADS // count
    groups = q_heads // kv_heads
    q_cols, kv_cols, ff_cols = q_heads * HEAD_SIZE, kv_heads * HEAD_SIZE, FF // count

    def shards(
        block_input,
        positions,
        out_cotangent,
        gain_attn,
        gain_ffn,
        w_query,
        w_key,
        value_weight,
        w_output,
        w_gate,
        w_up,
        w_down,
    ):
        tokens = block_input.shape[1]
        every = tokens * count
        index = lax.axis_index("ctx")

        def mine(weight, width):
            return lax.dynamic_slice_in_dim(weight, index * width, width, axis=1)

        gains = jnp.pad(jnp.stack([gain_attn, gain_ffn], axis=1), ((0, 0), (0, 126)))
        qkv_part = jnp.concatenate(
            [mine(w_query, q_cols), mine(w_key, kv_cols), mine(value_weight, kv_cols), gains], axis=1
        )
        gu_part = jnp.concatenate([mine(w_gate, ff_cols), mine(w_up, ff_cols)], axis=1)
        w_gu = lax.all_gather(gu_part, ROWS, axis=0, tiled=True)
        qkv_full = grid.gather_rows(qkv_part)
        w_o = grid.gather_rows(mine(w_output, q_cols))
        w_d = grid.gather_rows(mine(w_down, ff_cols))

        own_x = block_input[0]
        x_all = jnp.concatenate(ctx.gather(own_x), axis=0)
        order_all = jnp.concatenate(ctx.gather(positions[0]), axis=0)
        cotangent = out_cotangent[0]
        cot_all = jnp.concatenate(ctx.gather(cotangent), axis=0)

        qkv_cols = q_cols + 2 * kv_cols
        w_qkv = qkv_full[:, :qkv_cols]
        picks = (
            lax.broadcasted_iota(jnp.int32, (8, 128), 0)
            == lax.broadcasted_iota(jnp.int32, (8, 128), 1)
        ).astype(jnp.bfloat16)
        gains_full = times_t(picks, qkv_full[:, qkv_cols:])
        gain_first, gain_second = gains_full[0], gains_full[1]

        values_in = x_all.astype(jnp.float32)
        inverse_one = lax.rsqrt(jnp.mean(values_in * values_in, axis=1, keepdims=True) + EPSILON)
        normed_one = (values_in * inverse_one * gain_first[None, :]).astype(jnp.bfloat16)
        qkv = dot(w_qkv, normed_one, 0, 1)
        cosine_table, sine_values = rope_tables(order_all, HEAD_SIZE)
        attend, attend_backward = attention_calls(q_heads, groups, tokens, every)
        in_order, attended, lse = attend(order_all, qkv, cosine_table, sine_values)

        def split(full):
            return [full[j * tokens : (j + 1) * tokens] for j in range(count)]

        projected = ctx.reduce(split(dot(attended, w_o, 0, 1)))
        own_values = own_x.astype(jnp.float32)
        mid = own_values + projected
        inverse_two = lax.rsqrt(jnp.mean(mid * mid, axis=1, keepdims=True) + EPSILON)
        norm_two = mid * inverse_two
        normed_two = jnp.concatenate(
            ctx.gather((norm_two * gain_second[None, :]).astype(jnp.bfloat16)), axis=0
        )

        gate_up = times(normed_two, w_gu)
        d_hidden = times(cot_all, w_d)
        gate, up = gate_up[:, :ff_cols], gate_up[:, ff_cols:]
        sigma = jax.nn.sigmoid(gate)
        silu_gate = gate * sigma
        hidden = (silu_gate * up).astype(jnp.bfloat16)
        d_gate = (d_hidden * up * sigma * (1.0 + gate * (1.0 - sigma))).astype(jnp.bfloat16)
        d_up = (d_hidden * silu_gate).astype(jnp.bfloat16)
        d_gate_up = jnp.concatenate([d_gate, d_up], axis=1)
        d_normed_partial = times_t(d_gate_up, w_gu)
        grad_gu, d_normed_partial = lax.optimization_barrier(
            (left_t(normed_two, d_gate_up).astype(jnp.bfloat16), d_normed_partial)
        )
        d_normed_two = ctx.reduce(split(d_normed_partial))
        d_mid = cotangent.astype(jnp.float32) + norm_backward(
            d_normed_two, gain_second, norm_two, inverse_two
        )
        d_mid_b = jnp.concatenate(ctx.gather(d_mid.astype(jnp.bfloat16)), axis=0)

        grad_gu_rows = rows_scatter(grad_gu)
        grad_d_rows = grid.reduce_rows(left_t(cot_all, hidden))
        block_output = (mid + ctx.reduce(split(times_t(hidden, w_d)))).astype(jnp.bfloat16)

        d_attended = dot(w_o, d_mid_b, 0, 1).astype(jnp.bfloat16)
        d_qkv = attend_backward(
            order_all, in_order, lse, attended, d_attended, cosine_table, sine_values
        )
        d_normed_one = ctx.reduce(split(dot(d_qkv, w_qkv, 0, 1)))
        own_inverse = inverse_one[:tokens]
        input_grad = d_mid + norm_backward(
            d_normed_one, gain_first, own_values * own_inverse, own_inverse
        )

        grad_qkv_rows = grid.reduce_rows(dot(normed_one, d_qkv, 0, 1))
        grad_o_rows = grid.reduce_rows(dot(d_mid_b, attended, 0, 1))

        def spread(rows):
            return canonical(ctx.gather(rows), index)

        def joined(blocks, start, width):
            return jnp.concatenate(
                [b[:, start : start + width] for b in blocks], axis=1
            ).astype(jnp.float32)

        gu_blocks = spread(grad_gu_rows)
        grad_gate = joined(gu_blocks, 0, ff_cols)
        grad_up = joined(gu_blocks, ff_cols, ff_cols)
        grad_down = joined(spread(grad_d_rows), 0, ff_cols)
        attn_blocks = spread(grad_qkv_rows)
        grad_query = joined(attn_blocks, 0, q_cols)
        grad_key = joined(attn_blocks, q_cols, kv_cols)
        grad_value = joined(attn_blocks, q_cols + kv_cols, kv_cols)
        grad_output = joined(spread(grad_o_rows), 0, q_cols)

        grad_gain_attn = (
            jnp.sum(w_query.astype(jnp.float32) * grad_query, axis=1)
            + jnp.sum(w_key.astype(jnp.float32) * grad_key, axis=1)
            + jnp.sum(value_weight.astype(jnp.float32) * grad_value, axis=1)
        ) / gain_attn.astype(jnp.float32)
        grad_gain_ffn = (
            jnp.sum(w_gate.astype(jnp.float32) * grad_gate, axis=1)
            + jnp.sum(w_up.astype(jnp.float32) * grad_up, axis=1)
        ) / gain_ffn.astype(jnp.float32)
        return (
            block_output[None],
            input_grad[None],
            grad_gain_attn,
            grad_gain_ffn,
            grad_query,
            grad_key,
            grad_value,
            grad_output,
            grad_gate,
            grad_up,
            grad_down,
        )

    return shards


def solution(mesh):
    token, rows, matrix = P(ROWS, "ctx", None), P(ROWS), P(ROWS, None)
    return jax.shard_map(
        make(mesh),
        mesh=mesh,
        in_specs=(token, P(ROWS, "ctx"), token, rows, rows) + (matrix,) * 7,
        out_specs=(token, token, rows, rows) + (matrix,) * 7,
        check_vma=False,
    )
```
